32 devices in a mesh: re: 8 (over y, x, core), rp: 4 (over z).
Axes of the slice: x: 2, y: 2, z: 4, core: 2. Of those that a mesh axis runs over, the one named last changes fastest.
Arguments:
- wannier_table: bfloat16 [1024, 128, 1536], P('re', 'rp'), may hold values from -0.0078125 to 0.0078125
- mode_matrix: float32 [2, 12, 12], replicated, may hold values from -1.75 to 1.75
- re_coords: int32 [3, 1024], replicated, may hold values from -8 to 8
- rp_coords: int32 [3, 128], P(None, 'rp'), may hold values from -6 to 6
- q_coords: int32 [3, 2], replicated, may hold values from 0 to 63
- k_coords: int32 [3, 4096], P(None, 're'), may hold values from 0 to 63
- rotations: bfloat16 [4096, 128], P('re'), may hold values from -1.5 to 1.5
- kq_owner: int32 [2, 4096, 1], P(None, 're'), may hold values from 0 to 7; in each aligned block of 512 rows (0 to 511, 512 to 1023, ..., all dimensions but the last counted through in order) at most 96 rows name the same one
- kq_row: int32 [2, 4096], P(None, 're'), may hold values from 0 to 511
Outputs:
- couplings: bfloat16 [2, 12, 2, 64, 4096], P(None, 'rp', None, None, 're')
The draws below stay inside these ranges and needn't reach their ends.
Inputs may be any that keep to these rules, and one draw needn't show every extreme that they name: `kq_owner`: for each wavevector, among the 512 k-rows of one device no owner is named more than 96 times, a bound that some block reaches.
All inputs are finite; a program needn't handle non-finite values.
Results may differ from the reference program's by a relative error of at most 0.0057.
Values may be sent and summed in bfloat16 or wider, within the bound.
A program may use at most 128 MiB of HBM per device.

```python
import math
import jax
import jax.numpy as jnp
import numpy as np
from jax import lax

RE = 1024
RP = 128
NB = 8
MODES = 12
Q = 2
GRID = 64
K_DEV = 512
KPTS = 4096
CAP = 96
N_RE = 8


def touch_ends(array, own_key, smallest, largest):
    spot = [jax.random.randint(jax.random.fold_in(own_key, axis), (), 0, length) for axis, length in enumerate(array.shape)]
    main_axis = array.shape.index(max(array.shape))
    next_to = spot[:main_axis] + [(spot[main_axis] + 1) % array.shape[main_axis]] + spot[main_axis + 1:]
    return array.at[tuple(spot)].set(smallest).at[tuple(next_to)].set(largest)


def steps_of(key, dims, cuts, smallest, top_value):
    gain, own = 1.0, jax.random.fold_in(key, 6)
    for dim, blocks in cuts:
        heights = jnp.exp(jax.random.uniform(jax.random.fold_in(own, dim), (blocks,), jnp.float32, smallest / len(cuts), top_value / len(cuts)))
        gain = gain * jnp.repeat(heights, dims[dim] // blocks).reshape([-1 if axis == dim else 1 for axis in range(len(dims))])
    return gain


def deal_out(rng, own, number, rows, number_of, top, limit, lean):
    order = jax.random.permutation(rng, number_of)
    crowded, common = portions_of(number_of, rows * top, limit, lean, True), portions_of(number_of, rows * top, limit, lean, False)
    places = jnp.arange(number_of)

    def named(tallies, turn):
        used = int((tallies > 0).sum())
        fixed = max(1, used // 4)
        moved = fixed + (places - fixed + turn * (used - fixed)) % max(1, number_of - fixed)
        return jnp.zeros((number_of,), jnp.int32).at[order[jnp.where(places < fixed, places, moved)]].set(jnp.asarray(tallies, jnp.int32))

    tallies = jnp.where(number % 4 == 0, named(crowded, number // 4), named(common, number - number // 4 - 1))
    mixed = jax.random.permutation(jax.random.fold_in(own, 3), number_of)
    giver, sink = mixed[0:number_of // 2 * 2:2], mixed[1:number_of // 2 * 2:2]
    slack = jnp.minimum(tallies[giver] - 1, limit - tallies[sink]) // 2
    slack = jnp.where((giver == order[0]) | (sink == order[0]) | (tallies[sink] == 0), 0, jnp.maximum(slack, 0))
    moved = jax.random.randint(jax.random.fold_in(own, 4), (number_of // 2,), 0, 1 << 20) % (slack + 1)
    tallies = tallies.at[giver].add(-moved).at[sink].add(moved)
    items = jnp.searchsorted(jnp.cumsum(tallies), jnp.arange(rows * top), side="right").astype(jnp.int32)
    listing = items.reshape(top, rows).T
    listing = listing[jax.random.permutation(jax.random.fold_in(own, 1), rows)]
    turn = jax.random.randint(jax.random.fold_in(own, 2), (rows, 1), 0, top)
    return jnp.take_along_axis(listing, (jnp.arange(top)[None, :] + turn) % top, axis=1)


def portions_of(count, total, most, slope, full):
    weights = [(1 << 20) // math.isqrt(grade ** slope) + 1 for grade in range(1, count + 1)]
    largest = most if full else min(most, max(-(-total // count), total * weights[0] // sum(weights)))
    least = 1 if total - largest >= count - 1 else 0
    counts, spare = [largest] + [least] * (count - 1), total - largest - least * (count - 1)
    while spare > 0:
        candidates = [i for i in range(1, count) if counts[i] < largest] or [i for i in range(1, count) if counts[i] < most]
        whole, budget = sum([weights[i] for i in candidates]), spare
        for i in candidates:
            more = min(most - counts[i], max(1, budget * weights[i] // whole), spare)
            counts[i] = counts[i] + more
            spare = spare - more
    return np.array(counts)


def bell_draw(rng, extent, scale, reach, split=(), kind=jnp.bfloat16):
    factor_of = steps_of(rng, extent, split, -0.22, 0.18) if split else 1.0
    entries = jax.random.normal(rng, extent, jnp.float32) * scale * factor_of
    return jnp.minimum(jnp.maximum(entries, -reach), reach).astype(kind)


def setup_inputs(seed: int = 0) -> dict:
    arg_keys = jax.random.split(jax.random.key(seed), 10)
    wannier_table = bell_draw(arg_keys[0], (RE, RP, 2 * MODES * NB * NB), (4 * RP * RE) ** -0.5, 0.0078125, ((0, 8), (1, 4)))
    mode_matrix = bell_draw(arg_keys[1], (Q, MODES, MODES), MODES ** -0.5, 1.75, (), jnp.float32)
    re_coords = touch_ends(jax.random.randint(arg_keys[2], (3, RE), -8, 9), jax.random.fold_in(arg_keys[2], 1), -8, 8).astype(jnp.int32)
    rp_coords = touch_ends(jax.random.randint(arg_keys[3], (3, RP), -6, 7), jax.random.fold_in(arg_keys[3], 1), -6, 6).astype(jnp.int32)
    q_coords = touch_ends(jax.random.randint(arg_keys[4], (3, Q), 0, GRID), jax.random.fold_in(arg_keys[4], 1), 0, GRID - 1).astype(jnp.int32)
    k_coords = touch_ends(jax.random.randint(arg_keys[5], (3, KPTS), 0, GRID), jax.random.fold_in(arg_keys[5], 1), 0, GRID - 1).astype(jnp.int32)
    rotations = bell_draw(arg_keys[6], (KPTS, 2 * NB * NB), (2 * NB) ** -0.5, 1.5, ((0, 8),))
    kq_owner_keys = jax.random.split(jax.random.fold_in(arg_keys[7], 1), Q * KPTS // K_DEV)
    kq_owner_turns = jax.random.permutation(jax.random.fold_in(arg_keys[7], 3), Q * KPTS // K_DEV)
    kq_owner = jax.vmap(lambda own, number: deal_out(jax.random.fold_in(arg_keys[7], 2), own, number, K_DEV, N_RE, 1, CAP, 1))(kq_owner_keys, kq_owner_turns).reshape((Q, KPTS, 1))
    kq_row = touch_ends(jax.random.randint(arg_keys[8], (Q, KPTS), 0, K_DEV), jax.random.fold_in(arg_keys[8], 1), 0, K_DEV - 1).astype(jnp.int32)
    return dict(wannier_table=wannier_table, mode_matrix=mode_matrix, re_coords=re_coords, rp_coords=rp_coords, q_coords=q_coords, k_coords=k_coords, rotations=rotations, kq_owner=kq_owner, kq_row=kq_row)


def phases(left, right):
    products = jnp.sum(left[:, :, None] * right[:, None, :], axis=0)
    angles = jnp.mod(products, GRID).astype(jnp.float32) * (2.0 * math.pi / GRID)
    return jnp.cos(angles).astype(jnp.bfloat16), jnp.sin(angles).astype(jnp.bfloat16)


def rotate(coupling, right_rot, left_rot):
    highest = lax.Precision.HIGHEST
    coupling_real = coupling[:, :, 0]
    coupling_imag = coupling[:, :, 1]
    right_real = right_rot[0]
    right_imag = right_rot[1]
    half_real = jnp.einsum("qvabk,bnk->qvank", coupling_real, right_real, precision=highest) - jnp.einsum("qvabk,bnk->qvank", coupling_imag, right_imag, precision=highest)
    half_imag = jnp.einsum("qvabk,bnk->qvank", coupling_real, right_imag, precision=highest) + jnp.einsum("qvabk,bnk->qvank", coupling_imag, right_real, precision=highest)
    left_real = left_rot[:, 0]
    left_imag = left_rot[:, 1]
    result_real = jnp.einsum("qamk,qvank->qvmnk", left_real, half_real, precision=highest) + jnp.einsum("qamk,qvank->qvmnk", left_imag, half_imag, precision=highest)
    result_imag = jnp.einsum("qamk,qvank->qvmnk", left_real, half_imag, precision=highest) - jnp.einsum("qamk,qvank->qvmnk", left_imag, half_real, precision=highest)
    return jnp.stack([result_real, result_imag], axis=2)


def reference(wannier_table, mode_matrix, re_coords, rp_coords, q_coords, k_coords, rotations, kq_owner, kq_row):
    highest = lax.Precision.HIGHEST
    cosine_q, sine_q = phases(q_coords, rp_coords)
    cosine_q = cosine_q.astype(jnp.float32)
    sine_q = sine_q.astype(jnp.float32)
    re_block = min(128, RE)
    width = MODES * NB * NB

    def rp_block(table_rows):
        values = table_rows.reshape(re_block, RP, 2, width).astype(jnp.float32)
        with_cos = jnp.einsum("qr,ercw->eqcw", cosine_q, values, precision=highest)
        with_sin = jnp.einsum("qr,ercw->eqcw", sine_q, values, precision=highest)
        summed = jnp.stack([with_cos[:, :, 0] - with_sin[:, :, 1], with_sin[:, :, 0] + with_cos[:, :, 1]], axis=2)
        summed = summed.reshape(re_block, Q, 2, MODES, NB * NB)
        return jnp.einsum("eqcmz,qmn->eqcnz", summed, mode_matrix, precision=highest)

    mixed = lax.map(rp_block, wannier_table.reshape(RE // re_block, re_block, RP, 2 * width))
    mixed = mixed.reshape(RE, Q, 2, width)
    coupling_q = lax.optimization_barrier(mixed.astype(jnp.bfloat16)).astype(jnp.float32)
    k_block = 512

    def one_block(block_index):
        first_row = block_index * k_block
        block_coords = lax.dynamic_slice_in_dim(k_coords, first_row, k_block, 1)
        cosine_k, sine_k = phases(re_coords, block_coords)
        cosine_k = cosine_k.astype(jnp.float32)
        sine_k = sine_k.astype(jnp.float32)
        with_cos = jnp.einsum("eqcz,ek->qczk", coupling_q, cosine_k, precision=highest)
        with_sin = jnp.einsum("eqcz,ek->qczk", coupling_q, sine_k, precision=highest)
        coupling = jnp.stack([with_cos[:, 0] - with_sin[:, 1], with_sin[:, 0] + with_cos[:, 1]], axis=1)
        coupling = coupling.reshape(Q, 2, MODES, NB, NB, k_block).transpose(0, 2, 1, 3, 4, 5)
        local_rows = lax.dynamic_slice_in_dim(rotations, first_row, k_block, 0)
        local_rot = local_rows.astype(jnp.float32).T.reshape(2, NB, NB, k_block)
        owners = lax.dynamic_slice_in_dim(kq_owner[:, :, 0], first_row, k_block, 1)
        far_rows = lax.dynamic_slice_in_dim(kq_row, first_row, k_block, 1)
        positions = (owners * K_DEV + far_rows).astype(jnp.int32)
        far_rotation = rotations[positions]
        far_rot = far_rotation.astype(jnp.float32).transpose(0, 2, 1).reshape(Q, 2, NB, NB, k_block)
        result = rotate(coupling, local_rot, far_rot)
        return result.reshape(Q, MODES, 2, NB * NB, k_block).astype(jnp.bfloat16)

    blocks = lax.map(one_block, jnp.arange(KPTS // k_block, dtype=jnp.int32))
    return blocks.transpose(1, 2, 3, 4, 0, 5).reshape(Q, MODES, 2, NB * NB, KPTS)
```

```python
import functools
import math

import jax
import jax.numpy as jnp
from jax import lax
from jax.experimental import pallas as pl
from jax.experimental.pallas import tpu as pltpu
from jax.sharding import PartitionSpec as P

NB = 8
MODES = 12
Q = 2
GRID = 64
GROUP = 8
F32 = jnp.float32
BF16 = jnp.bfloat16


def phases(left, right):
    products = jnp.sum(left[:, :, None] * right[:, None, :], axis=0)
    angles = jnp.mod(products, GRID).astype(F32) * (2.0 * math.pi / GRID)
    return (jnp.cos(angles).astype(BF16), jnp.sin(angles).astype(BF16))


def sine_turn(turn):
    x = turn * (2.0 * math.pi)
    y = x * x
    p = 2.75573192e-6 - y * 2.50521084e-8
    p = -1.98412698e-4 + y * p
    p = 8.33333333e-3 + y * p
    p = -1.66666667e-1 + y * p
    return x + x * (y * p)


def mix_kernel(phase_ref, modes_ref, table_ref, out_ref, summed, kron):
    step = pl.program_id(0)
    block, r_local, both = table_ref.shape
    width = both // 2
    e_local = summed.shape[1] // 2
    owners, _, depth, _ = out_ref.shape

    @pl.when(step == 0)
    def _():
        shape = (MODES, width)
        expand = (
            lax.broadcasted_iota(jnp.int32, shape, 1) // (NB * NB)
            == lax.broadcasted_iota(jnp.int32, shape, 0)
        ).astype(F32).astype(BF16)
        rows = lax.broadcasted_iota(jnp.int32, (width, width), 0) & (NB * NB - 1)
        cols = lax.broadcasted_iota(jnp.int32, (width, width), 1) & (NB * NB - 1)
        for q in range(Q):
            spread = jnp.dot(modes_ref[q], expand, preferred_element_type=F32)
            kron[q] = jnp.where(rows == cols, spread, 0.0).astype(BF16)

    parts = []
    for g in range(block // GROUP):
        values = table_ref[g * GROUP : (g + 1) * GROUP].reshape(GROUP * r_local, both)
        parts.append(
            jnp.dot(phase_ref[0], values[:, :width], preferred_element_type=F32)
            + jnp.dot(phase_ref[1], values[:, width:], preferred_element_type=F32)
        )
    for q in range(Q):
        for c in range(2):
            first = (q * 2 + c) * GROUP
            rows = jnp.concatenate([part[first : first + GROUP] for part in parts], axis=0)
            start = pl.multiple_of(c * e_local + step * block, block)
            summed[q, pl.ds(start, block), :] = rows.astype(BF16)

    @pl.when(step == pl.num_programs(0) - 1)
    def _():
        for q in range(Q):
            mixed = lax.dot_general(
                kron[q], summed[q], (((1,), (1,)), ((), ())), preferred_element_type=F32
            ).astype(out_ref.dtype)
            for owner in range(owners):
                out_ref[owner, q] = mixed[owner * depth : (owner + 1) * depth]


def mix(phase, modes, table, owners):
    e_local, r_local, both = table.shape
    width = both // 2
    block = 16
    out_shape = (owners, Q, width // owners, 2 * e_local)
    return pl.pallas_call(
        mix_kernel,
        grid=(e_local // block,),
        in_specs=[
            pl.BlockSpec(phase.shape, lambda i: (0, 0, 0)),
            pl.BlockSpec(modes.shape, lambda i: (0, 0, 0)),
            pl.BlockSpec((block, r_local, both), lambda i: (i, 0, 0)),
        ],
        out_specs=pl.BlockSpec(out_shape, lambda i: (0, 0, 0, 0)),
        out_shape=jax.ShapeDtypeStruct(out_shape, BF16),
        scratch_shapes=[
            pltpu.VMEM((Q, 2 * e_local, width), BF16),
            pltpu.VMEM((Q, width, width), BF16),
        ],
        compiler_params=pltpu.CompilerParams(vmem_limit_bytes=40 << 20),
    )(phase, modes, table)


def bloch_kernel(
    coupling_ref, re_ref, k_ref, near_ref, all_ref, owner_ref, row_ref, out_ref,
    cosine, sine, summed, near, far,
):
    devices, _, depth, twice = coupling_ref.shape
    e_local = twice // 2
    k_local = k_ref.shape[1]
    modes_local = depth // (NB * NB)
    pairs = NB * NB
    near[...] = near_ref[...].astype(F32)

    @pl.loop(0, Q)
    def _(q):
        rows = lax.broadcasted_iota(jnp.int32, (k_local, k_local), 0)
        hot = (rows == row_ref[q]).astype(F32).astype(BF16)
        owner = owner_ref[q]
        far[q] = jnp.zeros(far.shape[1:], F32)

        @pl.loop(0, devices)
        def _(d):
            found = jnp.dot(all_ref[d], hot, preferred_element_type=F32)
            far[q] = jnp.where(owner == d, found, far[q])

    @pl.loop(0, devices)
    def _(d):
        start = pl.multiple_of(d * e_local, e_local)
        turns = jnp.dot(
            re_ref[pl.ds(start, e_local), :], k_ref[...], preferred_element_type=F32
        ) * (1.0 / GRID)
        turns = turns - jnp.floor(turns + 0.5)
        cosine[pl.ds(start, e_local), :] = sine_turn(0.25 - jnp.abs(turns)).astype(BF16)
        folded = jnp.maximum(jnp.minimum(turns, 0.5 - turns), -0.5 - turns)
        sine[pl.ds(start, e_local), :] = sine_turn(folded).astype(BF16)

    tile = min(256, k_local)

    @pl.loop(0, Q)
    def _(q):
        left = jnp.concatenate(
            [
                jnp.concatenate([coupling_ref[d, q, :, :e_local] for d in range(devices)], axis=1),
                jnp.concatenate([coupling_ref[d, q, :, e_local:] for d in range(devices)], axis=1),
            ],
            axis=0,
        )

        @pl.loop(0, k_local // tile)
        def _(j):
            cols = pl.ds(pl.multiple_of(j * tile, tile), tile)
            with_cos = jnp.dot(left, cosine[:, cols], preferred_element_type=F32)
            with_sin = jnp.dot(left, sine[:, cols], preferred_element_type=F32)
            real = with_cos[:depth] - with_sin[depth:]
            imag = with_cos[depth:] + with_sin[:depth]
            for v in range(modes_local):
                summed[q, 0, v, :, cols] = real[v * pairs : (v + 1) * pairs]
                summed[q, 1, v, :, cols] = imag[v * pairs : (v + 1) * pairs]

    lanes = 128
    tiles = k_local // lanes

    @pl.loop(0, Q * modes_local * tiles)
    def _(i):
        q = i // (modes_local * tiles)
        v = (i // tiles) % modes_local
        cols = pl.ds(pl.multiple_of((i % tiles) * lanes, lanes), lanes)

        def spread(ref, lead, row):
            return jnp.broadcast_to(ref[lead + (pl.ds(row, 1), cols)], (NB, lanes))

        right_real = [near[pl.ds(b * NB, NB), cols] for b in range(NB)]
        right_imag = [near[pl.ds(pairs + b * NB, NB), cols] for b in range(NB)]
        half_real, half_imag = [], []
        for a in range(NB):
            real = imag = None
            for b in range(NB):
                c_real = spread(summed, (q, 0, v), a * NB + b)
                c_imag = spread(summed, (q, 1, v), a * NB + b)
                one = c_real * right_real[b] - c_imag * right_imag[b]
                two = c_real * right_imag[b] + c_imag * right_real[b]
                real = one if real is None else real + one
                imag = two if imag is None else imag + two
            half_real.append(real)
            half_imag.append(imag)
        for m in range(0, NB, 2):
            reals, imags = [], []
            for n in (m, m + 1):
                real = imag = None
                for a in range(NB):
                    l_real = spread(far, (q,), a * NB + n)
                    l_imag = spread(far, (q,), pairs + a * NB + n)
                    one = l_real * half_real[a] + l_imag * half_imag[a]
                    two = l_real * half_imag[a] - l_imag * half_real[a]
                    real = one if real is None else real + one
                    imag = two if imag is None else imag + two
                reals.append(real)
                imags.append(imag)
            rows = pl.ds(m * NB, 2 * NB)
            out_ref[q, v, 0, rows, cols] = jnp.concatenate(reals, axis=0).astype(BF16)
            out_ref[q, v, 1, rows, cols] = jnp.concatenate(imags, axis=0).astype(BF16)


def bloch(coupling, re_rows, k_cols, near, everyone, owner, row):
    devices, _, depth, _ = coupling.shape
    e_all = re_rows.shape[0]
    k_local = k_cols.shape[1]
    modes_local = depth // (NB * NB)
    return pl.pallas_call(
        bloch_kernel,
        in_specs=[pl.BlockSpec(memory_space=pltpu.VMEM)] * 7,
        out_specs=pl.BlockSpec(memory_space=pltpu.VMEM),
        out_shape=jax.ShapeDtypeStruct((Q, modes_local, 2, NB * NB, k_local), BF16),
        scratch_shapes=[
            pltpu.VMEM((e_all, k_local), BF16),
            pltpu.VMEM((e_all, k_local), BF16),
            pltpu.VMEM((Q, 2, modes_local, NB * NB, k_local), F32),
            pltpu.VMEM((2 * NB * NB, k_local), F32),
            pltpu.VMEM((Q, 2 * NB * NB, k_local), F32),
        ],
        compiler_params=pltpu.CompilerParams(vmem_limit_bytes=56 << 20),
    )(coupling, re_rows, k_cols, near, everyone, owner, row)


def local(
    wannier_table,
    mode_matrix,
    re_coords,
    rp_coords,
    q_coords,
    k_coords,
    rotations,
    kq_owner,
    kq_row,
):
    e_local, r_local, _ = wannier_table.shape
    k_local = k_coords.shape[1]
    pairs = NB * NB
    cosine_q, sine_q = phases(q_coords, rp_coords)
    weights = jnp.stack(
        [jnp.stack([cosine_q, sine_q], axis=1), jnp.stack([-sine_q, cosine_q], axis=1)]
    )
    eye = jnp.eye(GROUP, dtype=BF16)
    phase = weights[:, :, :, None, None, :] * eye[None, None, None, :, :, None]
    phase = phase.reshape(2, Q * 2 * GROUP, GROUP * r_local)
    modes = jnp.repeat(mode_matrix.transpose(0, 2, 1).astype(BF16), pairs, axis=1)
    near = rotations.T
    everyone = lax.all_gather(near, "re", axis=0)
    partial = mix(phase, modes, wannier_table, lax.axis_size("rp"))
    owned = lax.psum_scatter(partial, "rp", scatter_dimension=0)
    coupling = lax.all_gather(owned, "re", axis=0)
    pad = ((0, 5), (0, 0))
    re_rows = jnp.pad(re_coords, pad).T.astype(BF16)
    k_cols = jnp.pad(k_coords, pad).astype(BF16)
    owner = kq_owner.reshape(Q, 1, k_local)
    row = kq_row.reshape(Q, 1, k_local)
    return bloch(coupling, re_rows, k_cols, near, everyone, owner, row)


def solution(mesh):
    in_specs = (
        P("re", "rp", None),
        P(),
        P(),
        P(None, "rp"),
        P(),
        P(None, "re"),
        P("re", None),
        P(None, "re", None),
        P(None, "re"),
    )
    out_specs = P(None, "rp", None, None, "re")
    return jax.shard_map(local, mesh=mesh, in_specs=in_specs, out_specs=out_specs, check_vma=False)
```

```python
import functools
import math

import jax
import jax.numpy as jnp
from jax import lax
from jax.experimental import pallas as pl
from jax.experimental.pallas import tpu as pltpu
from jax.sharding import PartitionSpec as P

NB = 8
MODES = 12
Q = 2
GRID = 64
GROUP = 8
F32 = jnp.float32
BF16 = jnp.bfloat16


def phases(left, right):
    products = jnp.sum(left[:, :, None] * right[:, None, :], axis=0)
    angles = jnp.mod(products, GRID).astype(F32) * (2.0 * math.pi / GRID)
    return (jnp.cos(angles).astype(BF16), jnp.sin(angles).astype(BF16))


def sine_turn(turn):
    x = turn * (2.0 * math.pi)
    y = x * x
    p = 2.75573192e-6 - y * 2.50521084e-8
    p = -1.98412698e-4 + y * p
    p = 8.33333333e-3 + y * p
    p = -1.66666667e-1 + y * p
    return x + x * (y * p)


def mix_kernel(phase_ref, modes_ref, table_ref, out_ref, summed, kron):
    step = pl.program_id(0)
    block, r_local, both = table_ref.shape
    width = both // 2
    e_local = summed.shape[1] // 2
    owners, _, depth, _ = out_ref.shape

    @pl.when(step == 0)
    def _():
        shape = (MODES, width)
        expand = (
            lax.broadcasted_iota(jnp.int32, shape, 1) // (NB * NB)
            == lax.broadcasted_iota(jnp.int32, shape, 0)
        ).astype(F32).astype(BF16)
        rows = lax.broadcasted_iota(jnp.int32, (width, width), 0) & (NB * NB - 1)
        cols = lax.broadcasted_iota(jnp.int32, (width, width), 1) & (NB * NB - 1)
        for q in range(Q):
            spread = jnp.dot(modes_ref[q], expand, preferred_element_type=F32)
            kron[q] = jnp.where(rows == cols, spread, 0.0).astype(BF16)

    parts = []
    for g in range(block // GROUP):
        values = table_ref[g * GROUP : (g + 1) * GROUP].reshape(GROUP * r_local, both)
        parts.append(
            jnp.dot(phase_ref[0], values[:, :width], preferred_element_type=F32)
            + jnp.dot(phase_ref[1], values[:, width:], preferred_element_type=F32)
        )
    for q in range(Q):
        for c in range(2):
            first = (q * 2 + c) * GROUP
            rows = jnp.concatenate([part[first : first + GROUP] for part in parts], axis=0)
            start = pl.multiple_of(c * e_local + step * block, block)
            summed[q, pl.ds(start, block), :] = rows.astype(BF16)

    @pl.when(step == pl.num_programs(0) - 1)
    def _():
        for q in range(Q):
            mixed = lax.dot_general(
                kron[q], summed[q], (((1,), (1,)), ((), ())), preferred_element_type=F32
            ).astype(out_ref.dtype)
            for owner in range(owners):
                out_ref[owner, q] = mixed[owner * depth : (owner + 1) * depth]


def mix(phase, modes, table, owners):
    e_local, r_local, both = table.shape
    width = both // 2
    block = 16
    out_shape = (owners, Q, width // owners, 2 * e_local)
    return pl.pallas_call(
        mix_kernel,
        grid=(e_local // block,),
        in_specs=[
            pl.BlockSpec(phase.shape, lambda i: (0, 0, 0)),
            pl.BlockSpec(modes.shape, lambda i: (0, 0, 0)),
            pl.BlockSpec((block, r_local, both), lambda i: (i, 0, 0)),
        ],
        out_specs=pl.BlockSpec(out_shape, lambda i: (0, 0, 0, 0)),
        out_shape=jax.ShapeDtypeStruct(out_shape, BF16),
        scratch_shapes=[
            pltpu.VMEM((Q, 2 * e_local, width), BF16),
            pltpu.VMEM((Q, width, width), BF16),
        ],
        compiler_params=pltpu.CompilerParams(vmem_limit_bytes=56 << 20),
    )(phase, modes, table)


MESH = pl.DeviceIdType.MESH


def send(source, target, send_sem, recv_sem, device):
    return pltpu.make_async_remote_copy(
        src_ref=source, dst_ref=target, send_sem=send_sem, recv_sem=recv_sem,
        device_id=device, device_id_type=MESH,
    )


def exchange_kernel(
    partial_ref, near_ref, coupling_ref, all_ref,
    inbox, sum_send, sum_recv, far_send, far_recv, pair_send, pair_recv,
):
    shares, _, depth, _ = partial_ref.shape
    half = coupling_ref.shape[0] // 2
    me, row = lax.axis_index("re"), lax.axis_index("rp")
    mate = me ^ 1
    chunks = sum_send.shape[0]
    rows = Q * depth // chunks

    barrier = pltpu.get_barrier_semaphore()
    peers = [(me, lax.rem(row + j, shares)) for j in range(1, shares)]
    peers += [(me ^ (2 * j), row) for j in range(1, half)] + [(mate, row)]
    for peer in peers:
        pl.semaphore_signal(barrier, inc=1, device_id=peer, device_id_type=MESH)
    pl.semaphore_wait(barrier, len(peers))

    def piece(c):
        q, first = divmod(c * rows, depth)
        return q, pl.ds(first, rows)

    waits = []
    sums = {}
    for c in range(chunks):
        at = piece(c)
        for j in range(1, shares):
            to = lax.rem(row + j, shares)
            copy = send(
                partial_ref.at[(to,) + at], inbox.at[(j - 1,) + at],
                sum_send.at[c, j - 1], sum_recv.at[c, j - 1], (me, to),
            )
            copy.start()
            sums[c, j] = copy

    def spread(c, block, whole):
        own = []
        for j in range(1, half):
            copy = send(
                block, whole(me), far_send.at[c, j], far_recv.at[c, j], (me ^ (2 * j), row)
            )
            copy.start()
            own.append(copy)
        copy = send(block, whole(me), pair_send.at[c, 0], pair_recv.at[c, 0], (mate, row))
        copy.start()
        waits.append(copy)
        return own

    def forward(c, own, whole):
        for j in range(1, half):
            own[j - 1].wait()
            block = whole(me ^ (2 * j))
            copy = send(block, block, pair_send.at[c, j], pair_recv.at[c, j], (mate, row))
            copy.start()
            waits.append(copy)

    def rotations_of(d):
        return all_ref.at[d]

    def coupling_of(c):
        at = piece(c)
        return lambda d: coupling_ref.at[(d,) + at]

    all_ref[me] = near_ref[...]
    spreads = [spread(chunks, near_ref, rotations_of)]
    wholes = [rotations_of]
    order = [chunks]
    for c in range(chunks):
        at = piece(c)
        total = partial_ref[(row,) + at].astype(F32)
        for j in range(1, shares):
            sums[c, j].wait()
            total = total + inbox[(j - 1,) + at].astype(F32)
        coupling_ref[(me,) + at] = total.astype(BF16)
        spreads.append(spread(c, coupling_of(c)(me), coupling_of(c)))
        wholes.append(coupling_of(c))
        order.append(c)
        forward(order[-2], spreads[-2], wholes[-2])
    forward(order[-1], spreads[-1], wholes[-1])
    for copy in waits:
        copy.wait()


def exchange(partial, near, devices):
    shares, _, depth, twice = partial.shape
    chunks = Q * 2
    half = devices // 2
    return pl.pallas_call(
        exchange_kernel,
        in_specs=[pl.BlockSpec(memory_space=pltpu.VMEM)] * 2,
        out_specs=[pl.BlockSpec(memory_space=pltpu.VMEM)] * 2,
        out_shape=[
            jax.ShapeDtypeStruct((devices, Q, depth, twice), BF16),
            jax.ShapeDtypeStruct((devices,) + near.shape, BF16),
        ],
        scratch_shapes=[
            pltpu.VMEM((shares - 1, Q, depth, twice), BF16),
            pltpu.SemaphoreType.DMA((chunks, shares - 1)),
            pltpu.SemaphoreType.DMA((chunks, shares - 1)),
            pltpu.SemaphoreType.DMA((chunks + 1, half)),
            pltpu.SemaphoreType.DMA((chunks + 1, half)),
            pltpu.SemaphoreType.DMA((chunks + 1, half)),
            pltpu.SemaphoreType.DMA((chunks + 1, half)),
        ],
        compiler_params=pltpu.CompilerParams(
            collective_id=0, has_side_effects=True, vmem_limit_bytes=16 << 20
        ),
    )(partial, near)


def bloch_kernel(
    coupling_ref, re_ref, k_ref, near_ref, all_ref, owner_ref, row_ref, out_ref,
    cosine, sine, summed, near, far,
):
    devices, _, depth, twice = coupling_ref.shape
    e_local = twice // 2
    k_local = k_ref.shape[1]
    modes_local = depth // (NB * NB)
    pairs = NB * NB
    near[...] = near_ref[...].astype(F32)

    @pl.loop(0, Q)
    def _(q):
        rows = lax.broadcasted_iota(jnp.int32, (k_local, k_local), 0)
        hot = (rows == row_ref[q]).astype(F32).astype(BF16)
        owner = owner_ref[q]
        far[q] = jnp.zeros(far.shape[1:], F32)

        @pl.loop(0, devices)
        def _(d):
            found = jnp.dot(all_ref[d], hot, preferred_element_type=F32)
            far[q] = jnp.where(owner == d, found, far[q])

    @pl.loop(0, devices)
    def _(d):
        start = pl.multiple_of(d * e_local, e_local)
        turns = jnp.dot(
            re_ref[pl.ds(start, e_local), :], k_ref[...], preferred_element_type=F32
        ) * (1.0 / GRID)
        turns = turns - jnp.floor(turns + 0.5)
        cosine[pl.ds(start, e_local), :] = sine_turn(0.25 - jnp.abs(turns)).astype(BF16)
        folded = jnp.maximum(jnp.minimum(turns, 0.5 - turns), -0.5 - turns)
        sine[pl.ds(start, e_local), :] = sine_turn(folded).astype(BF16)

    tile = min(256, k_local)

    @pl.loop(0, Q)
    def _(q):
        left = jnp.concatenate(
            [
                jnp.concatenate([coupling_ref[d, q, :, :e_local] for d in range(devices)], axis=1),
                jnp.concatenate([coupling_ref[d, q, :, e_local:] for d in range(devices)], axis=1),
            ],
            axis=0,
        )

        @pl.loop(0, k_local // tile)
        def _(j):
            cols = pl.ds(pl.multiple_of(j * tile, tile), tile)
            with_cos = jnp.dot(left, cosine[:, cols], preferred_element_type=F32)
            with_sin = jnp.dot(left, sine[:, cols], preferred_element_type=F32)
            real = with_cos[:depth] - with_sin[depth:]
            imag = with_cos[depth:] + with_sin[:depth]
            for v in range(modes_local):
                summed[q, 0, v, :, cols] = real[v * pairs : (v + 1) * pairs]
                summed[q, 1, v, :, cols] = imag[v * pairs : (v + 1) * pairs]

    lanes = 128
    tiles = k_local // lanes

    @pl.loop(0, Q * modes_local * tiles)
    def _(i):
        q = i // (modes_local * tiles)
        v = (i // tiles) % modes_local
        cols = pl.ds(pl.multiple_of((i % tiles) * lanes, lanes), lanes)

        def spread(ref, lead, row):
            return jnp.broadcast_to(ref[lead + (pl.ds(row, 1), cols)], (NB, lanes))

        right_real = [near[pl.ds(b * NB, NB), cols] for b in range(NB)]
        right_imag = [near[pl.ds(pairs + b * NB, NB), cols] for b in range(NB)]
        half_real, half_imag = [], []
        for a in range(NB):
            real = imag = None
            for b in range(NB):
                c_real = spread(summed, (q, 0, v), a * NB + b)
                c_imag = spread(summed, (q, 1, v), a * NB + b)
                one = c_real * right_real[b] - c_imag * right_imag[b]
                two = c_real * right_imag[b] + c_imag * right_real[b]
                real = one if real is None else real + one
                imag = two if imag is None else imag + two
            half_real.append(real)
            half_imag.append(imag)
        for m in range(0, NB, 2):
            reals, imags = [], []
            for n in (m, m + 1):
                real = imag = None
                for a in range(NB):
                    l_real = spread(far, (q,), a * NB + n)
                    l_imag = spread(far, (q,), pairs + a * NB + n)
                    one = l_real * half_real[a] + l_imag * half_imag[a]
                    two = l_real * half_imag[a] - l_imag * half_real[a]
                    real = one if real is None else real + one
                    imag = two if imag is None else imag + two
                reals.append(real)
                imags.append(imag)
            rows = pl.ds(m * NB, 2 * NB)
            out_ref[q, v, 0, rows, cols] = jnp.concatenate(reals, axis=0).astype(BF16)
            out_ref[q, v, 1, rows, cols] = jnp.concatenate(imags, axis=0).astype(BF16)


def bloch(coupling, re_rows, k_cols, near, everyone, owner, row):
    devices, _, depth, _ = coupling.shape
    e_all = re_rows.shape[0]
    k_local = k_cols.shape[1]
    modes_local = depth // (NB * NB)
    return pl.pallas_call(
        bloch_kernel,
        in_specs=[pl.BlockSpec(memory_space=pltpu.VMEM)] * 7,
        out_specs=pl.BlockSpec(memory_space=pltpu.VMEM),
        out_shape=jax.ShapeDtypeStruct((Q, modes_local, 2, NB * NB, k_local), BF16),
        scratch_shapes=[
            pltpu.VMEM((e_all, k_local), BF16),
            pltpu.VMEM((e_all, k_local), BF16),
            pltpu.VMEM((Q, 2, modes_local, NB * NB, k_local), F32),
            pltpu.VMEM((2 * NB * NB, k_local), F32),
            pltpu.VMEM((Q, 2 * NB * NB, k_local), F32),
        ],
        compiler_params=pltpu.CompilerParams(vmem_limit_bytes=24 << 20),
    )(coupling, re_rows, k_cols, near, everyone, owner, row)


def local(
    wannier_table,
    mode_matrix,
    re_coords,
    rp_coords,
    q_coords,
    k_coords,
    rotations,
    kq_owner,
    kq_row,
):
    e_local, r_local, _ = wannier_table.shape
    k_local = k_coords.shape[1]
    pairs = NB * NB
    cosine_q, sine_q = phases(q_coords, rp_coords)
    weights = jnp.stack(
        [jnp.stack([cosine_q, sine_q], axis=1), jnp.stack([-sine_q, cosine_q], axis=1)]
    )
    eye = jnp.eye(GROUP, dtype=BF16)
    phase = weights[:, :, :, None, None, :] * eye[None, None, None, :, :, None]
    phase = phase.reshape(2, Q * 2 * GROUP, GROUP * r_local)
    modes = jnp.repeat(mode_matrix.transpose(0, 2, 1).astype(BF16), pairs, axis=1)
    near = rotations.T
    partial = mix(phase, modes, wannier_table, lax.axis_size("rp"))
    coupling, everyone = exchange(partial, near, lax.axis_size("re"))
    pad = ((0, 5), (0, 0))
    re_rows = jnp.pad(re_coords, pad).T.astype(BF16)
    k_cols = jnp.pad(k_coords, pad).astype(BF16)
    owner = kq_owner.reshape(Q, 1, k_local)
    row = kq_row.reshape(Q, 1, k_local)
    return bloch(coupling, re_rows, k_cols, near, everyone, owner, row)


def solution(mesh):
    in_specs = (
        P("re", "rp", None),
        P(),
        P(),
        P(None, "rp"),
        P(),
        P(None, "re"),
        P("re", None),
        P(None, "re", None),
        P(None, "re"),
    )
    out_specs = P(None, "rp", None, None, "re")
    return jax.shard_map(local, mesh=mesh, in_specs=in_specs, out_specs=out_specs, check_vma=False)
```

```python
import functools
import math

import jax
import jax.numpy as jnp
from jax import lax
from jax.experimental import pallas as pl
from jax.experimental.pallas import tpu as pltpu
from jax.sharding import PartitionSpec as P

NB = 8
MODES = 12
Q = 2
GRID = 64
GROUP = 8
F32 = jnp.float32
BF16 = jnp.bfloat16


def phases(left, right):
    products = jnp.sum(left[:, :, None] * right[:, None, :], axis=0)
    angles = jnp.mod(products, GRID).astype(F32) * (2.0 * math.pi / GRID)
    return (jnp.cos(angles).astype(BF16), jnp.sin(angles).astype(BF16))


def sine_turn(turn):
    x = turn * (2.0 * math.pi)
    y = x * x
    p = 2.75573192e-6 - y * 2.50521084e-8
    p = -1.98412698e-4 + y * p
    p = 8.33333333e-3 + y * p
    p = -1.66666667e-1 + y * p
    return x + x * (y * p)


def mix_kernel(phase_ref, modes_ref, table_ref, out_ref, summed, kron):
    step = pl.program_id(0)
    block, r_local, both = table_ref.shape
    width = both // 2
    e_local = summed.shape[1] // 2
    owners, _, depth, _ = out_ref.shape

    @pl.when(step == 0)
    def _():
        shape = (MODES, width)
        expand = (
            lax.broadcasted_iota(jnp.int32, shape, 1) // (NB * NB)
            == lax.broadcasted_iota(jnp.int32, shape, 0)
        ).astype(F32).astype(BF16)
        rows = lax.broadcasted_iota(jnp.int32, (width, width), 0) & (NB * NB - 1)
        cols = lax.broadcasted_iota(jnp.int32, (width, width), 1) & (NB * NB - 1)
        for q in range(Q):
            spread = jnp.dot(modes_ref[q], expand, preferred_element_type=F32)
            kron[q] = jnp.where(rows == cols, spread, 0.0).astype(BF16)

    parts = []
    for g in range(block // GROUP):
        values = table_ref[g * GROUP : (g + 1) * GROUP].reshape(GROUP * r_local, both)
        parts.append(
            jnp.dot(phase_ref[0], values[:, :width], preferred_element_type=F32)
            + jnp.dot(phase_ref[1], values[:, width:], preferred_element_type=F32)
        )
    for q in range(Q):
        for c in range(2):
            first = (q * 2 + c) * GROUP
            rows = jnp.concatenate([part[first : first + GROUP] for part in parts], axis=0)
            start = pl.multiple_of(c * e_local + step * block, block)
            summed[q, pl.ds(start, block), :] = rows.astype(BF16)

    @pl.when(step == pl.num_programs(0) - 1)
    def _():
        for q in range(Q):
            mixed = lax.dot_general(
                kron[q], summed[q], (((1,), (1,)), ((), ())), preferred_element_type=F32
            ).astype(out_ref.dtype)
            for owner in range(owners):
                out_ref[owner, q] = mixed[owner * depth : (owner + 1) * depth]


def mix(phase, modes, table, owners):
    e_local, r_local, both = table.shape
    width = both // 2
    block = 16
    out_shape = (owners, Q, width // owners, 2 * e_local)
    return pl.pallas_call(
        mix_kernel,
        grid=(e_local // block,),
        in_specs=[
            pl.BlockSpec(phase.shape, lambda i: (0, 0, 0)),
            pl.BlockSpec(modes.shape, lambda i: (0, 0, 0)),
            pl.BlockSpec((block, r_local, both), lambda i: (i, 0, 0)),
        ],
        out_specs=pl.BlockSpec(out_shape, lambda i: (0, 0, 0, 0)),
        out_shape=jax.ShapeDtypeStruct(out_shape, BF16),
        scratch_shapes=[
            pltpu.VMEM((Q, 2 * e_local, width), BF16),
            pltpu.VMEM((Q, width, width), BF16),
        ],
        compiler_params=pltpu.CompilerParams(vmem_limit_bytes=50 << 20),
    )(phase, modes, table)


MESH = pl.DeviceIdType.MESH


def send(source, target, send_sem, recv_sem, device):
    return pltpu.make_async_remote_copy(
        src_ref=source, dst_ref=target, send_sem=send_sem, recv_sem=recv_sem,
        device_id=device, device_id_type=MESH,
    )


def bloch_kernel(
    partial_ref, near_ref, re_ref, k_ref, owner_ref, row_ref, out_ref,
    coupling_ref, all_ref, inbox, cosine, sine, summed, near, far,
    sum_send, sum_recv, far_send, far_recv, pair_send, pair_recv,
):
    shares = partial_ref.shape[0]
    devices, _, depth, twice = coupling_ref.shape
    half = devices // 2
    e_local = twice // 2
    k_local = k_ref.shape[1]
    pairs = NB * NB
    modes_local = depth // pairs
    chunks = Q * modes_local
    me, place = lax.axis_index("re"), lax.axis_index("rp")
    mate = me ^ 1

    barrier = pltpu.get_barrier_semaphore()
    peers = [(me, lax.rem(place + j, shares)) for j in range(1, shares)]
    peers += [(me ^ (2 * j), place) for j in range(1, half)] + [(mate, place)]
    for peer in peers:
        pl.semaphore_signal(barrier, inc=1, device_id=peer, device_id_type=MESH)
    pl.semaphore_wait(barrier, len(peers))

    def piece(c):
        q, v = divmod(c, modes_local)
        return q, pl.ds(v * pairs, pairs)

    sums = {}
    for c in range(chunks):
        at = piece(c)
        for j in range(1, shares):
            to = lax.rem(place + j, shares)
            copy = send(
                partial_ref.at[(to,) + at], inbox.at[(j - 1,) + at],
                sum_send.at[c, j - 1], sum_recv.at[c, j - 1], (me, to),
            )
            copy.start()
            sums[c, j] = copy

    spreads, waits, wholes = {}, {}, {}

    def spread(c, block, whole):
        wholes[c] = whole
        spreads[c] = []
        copy = send(block, whole(me), pair_send.at[c, 0], pair_recv.at[c, 0], (mate, place))
        for j in range(1, half):
            far_copy = send(
                block, whole(me), far_send.at[c, j], far_recv.at[c, j], (me ^ (2 * j), place)
            )
            far_copy.start()
            spreads[c].append(far_copy)
        copy.start()
        waits[c] = [copy]

    def forward(c):
        for j in range(1, half):
            spreads[c][j - 1].wait()
            block = wholes[c](me ^ (2 * j))
            copy = send(block, block, pair_send.at[c, j], pair_recv.at[c, j], (mate, place))
            copy.start()
            waits[c].append(copy)

    def collect(c):
        for copy in waits[c]:
            copy.wait()

    def add_up(c):
        at = piece(c)
        total = partial_ref[(place,) + at].astype(F32)
        for j in range(1, shares):
            sums[c, j].wait()
            total = total + inbox[(j - 1,) + at].astype(F32)
        coupling_ref[(me,) + at] = total.astype(BF16)
        whole = lambda d: coupling_ref.at[(d,) + at]
        spread(c, whole(me), whole)

    all_ref[me] = near_ref[...]
    spread(chunks, near_ref, lambda d: all_ref.at[d])

    near[...] = near_ref[...].astype(F32)

    @pl.loop(0, devices)
    def _(d):
        start = pl.multiple_of(d * e_local, e_local)
        turns = jnp.dot(
            re_ref[pl.ds(start, e_local), :], k_ref[...], preferred_element_type=F32
        ) * (1.0 / GRID)
        turns = turns - jnp.floor(turns + 0.5)
        cosine[pl.ds(start, e_local), :] = sine_turn(0.25 - jnp.abs(turns)).astype(BF16)
        folded = jnp.maximum(jnp.minimum(turns, 0.5 - turns), -0.5 - turns)
        sine[pl.ds(start, e_local), :] = sine_turn(folded).astype(BF16)

    def look_up(q):
        rows = lax.broadcasted_iota(jnp.int32, (k_local, k_local), 0)
        hot = (rows == row_ref[q]).astype(F32).astype(BF16)
        owner = owner_ref[q]
        far[q] = jnp.zeros(far.shape[1:], F32)

        @pl.loop(0, devices)
        def _(d):
            found = jnp.dot(all_ref[d], hot, preferred_element_type=F32)
            far[q] = jnp.where(owner == d, found, far[q])

    tile = min(256, k_local)
    lanes = 128

    def compute(c):
        q, v = divmod(c, modes_local)
        at = (q, pl.ds(v * pairs, pairs))
        left = jnp.concatenate(
            [
                jnp.concatenate(
                    [coupling_ref[(d,) + at][:, i * e_local : (i + 1) * e_local]
                     for d in range(devices)], axis=1,
                )
                for i in range(2)
            ],
            axis=0,
        )

        @pl.loop(0, k_local // tile)
        def _(j):
            cols = pl.ds(pl.multiple_of(j * tile, tile), tile)
            with_cos = jnp.dot(left, cosine[:, cols], preferred_element_type=F32)
            with_sin = jnp.dot(left, sine[:, cols], preferred_element_type=F32)
            summed[0, :, cols] = with_cos[:pairs] - with_sin[pairs:]
            summed[1, :, cols] = with_cos[pairs:] + with_sin[:pairs]

        @pl.loop(0, k_local // lanes)
        def _(i):
            cols = pl.ds(pl.multiple_of(i * lanes, lanes), lanes)

            def fill(ref, lead, row):
                return jnp.broadcast_to(ref[lead, pl.ds(row, 1), cols], (NB, lanes))

            right_real = [near[pl.ds(b * NB, NB), cols] for b in range(NB)]
            right_imag = [near[pl.ds(pairs + b * NB, NB), cols] for b in range(NB)]
            half_real, half_imag = [], []
            for a in range(NB):
                real = imag = None
                for b in range(NB):
                    c_real = fill(summed, 0, a * NB + b)
                    c_imag = fill(summed, 1, a * NB + b)
                    one = c_real * right_real[b] - c_imag * right_imag[b]
                    two = c_real * right_imag[b] + c_imag * right_real[b]
                    real = one if real is None else real + one
                    imag = two if imag is None else imag + two
                half_real.append(real)
                half_imag.append(imag)
            for m in range(0, NB, 2):
                reals, imags = [], []
                for n in (m, m + 1):
                    real = imag = None
                    for a in range(NB):
                        l_real = fill(far, q, a * NB + n)
                        l_imag = fill(far, q, pairs + a * NB + n)
                        one = l_real * half_real[a] + l_imag * half_imag[a]
                        two = l_real * half_imag[a] - l_imag * half_real[a]
                        real = one if real is None else real + one
                        imag = two if imag is None else imag + two
                    reals.append(real)
                    imags.append(imag)
                rows = pl.ds(m * NB, 2 * NB)
                out_ref[q, v, 0, rows, cols] = jnp.concatenate(reals, axis=0).astype(BF16)
                out_ref[q, v, 1, rows, cols] = jnp.concatenate(imags, axis=0).astype(BF16)

    lag = 3
    for t in range(chunks + lag):
        if t < chunks:
            add_up(t)
        if t == 0:
            forward(chunks)
        elif t <= chunks:
            forward(t - 1)
        if t == 1:
            collect(chunks)
        if 1 <= t <= Q:
            look_up(t - 1)
        if t >= lag:
            collect(t - lag)
            compute(t - lag)


def bloch(partial, near, re_rows, k_cols, owner, row, devices):
    shares, _, depth, twice = partial.shape
    e_all = re_rows.shape[0]
    k_local = k_cols.shape[1]
    pairs = NB * NB
    modes_local = depth // pairs
    chunks = Q * modes_local
    half = devices // 2
    return pl.pallas_call(
        bloch_kernel,
        in_specs=[pl.BlockSpec(memory_space=pltpu.VMEM)] * 6,
        out_specs=pl.BlockSpec(memory_space=pltpu.VMEM),
        out_shape=jax.ShapeDtypeStruct((Q, modes_local, 2, pairs, k_local), BF16),
        scratch_shapes=[
            pltpu.VMEM((devices, Q, depth, twice), BF16),
            pltpu.VMEM((devices,) + near.shape, BF16),
            pltpu.VMEM((shares - 1, Q, depth, twice), BF16),
            pltpu.VMEM((e_all, k_local), BF16),
            pltpu.VMEM((e_all, k_local), BF16),
            pltpu.VMEM((2, pairs, k_local), F32),
            pltpu.VMEM((2 * pairs, k_local), F32),
            pltpu.VMEM((Q, 2 * pairs, k_local), F32),
            pltpu.SemaphoreType.DMA((chunks, shares - 1)),
            pltpu.SemaphoreType.DMA((chunks, shares - 1)),
            pltpu.SemaphoreType.DMA((chunks + 1, half)),
            pltpu.SemaphoreType.DMA((chunks + 1, half)),
            pltpu.SemaphoreType.DMA((chunks + 1, half)),
            pltpu.SemaphoreType.DMA((chunks + 1, half)),
        ],
        compiler_params=pltpu.CompilerParams(
            collective_id=0, has_side_effects=True, vmem_limit_bytes=40 << 20
        ),
    )(partial, near, re_rows, k_cols, owner, row)


def local(
    wannier_table,
    mode_matrix,
    re_coords,
    rp_coords,
    q_coords,
    k_coords,
    rotations,
    kq_owner,
    kq_row,
):
    e_local, r_local, _ = wannier_table.shape
    k_local = k_coords.shape[1]
    pairs = NB * NB
    cosine_q, sine_q = phases(q_coords, rp_coords)
    weights = jnp.stack(
        [jnp.stack([cosine_q, sine_q], axis=1), jnp.stack([-sine_q, cosine_q], axis=1)]
    )
    eye = jnp.eye(GROUP, dtype=BF16)
    phase = weights[:, :, :, None, None, :] * eye[None, None, None, :, :, None]
    phase = phase.reshape(2, Q * 2 * GROUP, GROUP * r_local)
    modes = jnp.repeat(mode_matrix.transpose(0, 2, 1).astype(BF16), pairs, axis=1)
    near = rotations.T
    partial = mix(phase, modes, wannier_table, lax.axis_size("rp"))
    pad = ((0, 5), (0, 0))
    re_rows = jnp.pad(re_coords, pad).T.astype(BF16)
    k_cols = jnp.pad(k_coords, pad).astype(BF16)
    owner = kq_owner.reshape(Q, 1, k_local)
    row = kq_row.reshape(Q, 1, k_local)
    return bloch(partial, near, re_rows, k_cols, owner, row, lax.axis_size("re"))


def solution(mesh):
    in_specs = (
        P("re", "rp", None),
        P(),
        P(),
        P(None, "rp"),
        P(),
        P(None, "re"),
        P("re", None),
        P(None, "re", None),
        P(None, "re"),
    )
    out_specs = P(None, "rp", None, None, "re")
    return jax.shard_map(local, mesh=mesh, in_specs=in_specs, out_specs=out_specs, check_vma=False)
```

```python
import functools
import math

import jax
import jax.numpy as jnp
from jax import lax
from jax.experimental import pallas as pl
from jax.experimental.pallas import tpu as pltpu
from jax.sharding import PartitionSpec as P

NB = 8
MODES = 12
Q = 2
GRID = 64
GROUP = 8
F32 = jnp.float32
BF16 = jnp.bfloat16


def sine_turn(turn):
    x = turn * (2.0 * math.pi)
    y = x * x
    p = 2.75573192e-6 - y * 2.50521084e-8
    p = -1.98412698e-4 + y * p
    p = 8.33333333e-3 + y * p
    p = -1.66666667e-1 + y * p
    return x + x * (y * p)


def cycle(turns):
    turns = turns - jnp.floor(turns + 0.5)
    folded = jnp.maximum(jnp.minimum(turns, 0.5 - turns), -0.5 - turns)
    return sine_turn(0.25 - jnp.abs(turns)).astype(BF16), sine_turn(folded).astype(BF16)


def narrow(integers):
    return integers.astype(F32).astype(BF16)


def inner(left, right):
    return lax.dot_general(left, right, (((0,), (0,)), ((), ())), preferred_element_type=F32)


def iota(shape, dim):
    return lax.broadcasted_iota(jnp.int32, shape, dim)


def mix_kernel(rp_ref, q_ref, modes_ref, table_ref, out_ref, summed, kron, phase):
    pairs = NB * NB
    step = pl.program_id(0)
    block, r_local, both = table_ref.shape
    width = both // 2
    e_local = summed.shape[1] // 2
    owners, _, depth, _ = out_ref.shape

    @pl.when(step == 0)
    def _():
        lanes_in = GROUP * r_local
        tiling = (iota((r_local, lanes_in), 1) % r_local == iota((r_local, lanes_in), 0))
        tiled = jnp.dot(narrow(rp_ref[...]), narrow(tiling), preferred_element_type=F32)
        products = inner(narrow(q_ref[...]), tiled.astype(BF16))
        shape = (Q * 2 * GROUP, lanes_in)
        line = iota(shape, 0)
        spread_out = jnp.broadcast_to(products[0:1], shape)
        for q in range(1, Q):
            spread_out = jnp.where(line // (2 * GROUP) == q, products[q : q + 1], spread_out)
        cos_q, sin_q = cycle(spread_out * (1.0 / GRID))
        cos_q, sin_q = cos_q.astype(F32), sin_q.astype(F32)
        real = (line // GROUP) % 2 == 0
        same = line % GROUP == iota(shape, 1) // r_local
        phase[0] = jnp.where(same, jnp.where(real, cos_q, sin_q), 0.0).astype(BF16)
        phase[1] = jnp.where(same, jnp.where(real, -sin_q, cos_q), 0.0).astype(BF16)

        tall = narrow(iota((width, MODES), 0) // pairs == iota((width, MODES), 1))
        wide = narrow(iota((MODES, width), 1) // pairs == iota((MODES, width), 0))
        diagonal = iota((width, width), 0) % pairs == iota((width, width), 1) % pairs
        for q in range(Q):
            rows = lax.dot_general(
                tall, modes_ref[q].astype(BF16), (((1,), (1,)), ((), ())),
                preferred_element_type=F32,
            )
            full = jnp.dot(rows.astype(BF16), wide, preferred_element_type=F32)
            kron[q] = jnp.where(diagonal, full, 0.0).astype(BF16)

    parts = []
    for g in range(block // GROUP):
        values = table_ref[g * GROUP : (g + 1) * GROUP].reshape(GROUP * r_local, both)
        parts.append(
            jnp.dot(phase[0], values[:, :width], preferred_element_type=F32)
            + jnp.dot(phase[1], values[:, width:], preferred_element_type=F32)
        )
    for q in range(Q):
        for c in range(2):
            first = (q * 2 + c) * GROUP
            rows = jnp.concatenate([part[first : first + GROUP] for part in parts], axis=0)
            start = pl.multiple_of(c * e_local + step * block, block)
            summed[q, pl.ds(start, block), :] = rows.astype(BF16)

    @pl.when(step == pl.num_programs(0) - 1)
    def _():
        for q in range(Q):
            mixed = lax.dot_general(
                kron[q], summed[q], (((1,), (1,)), ((), ())), preferred_element_type=F32
            ).astype(out_ref.dtype)
            for owner in range(owners):
                out_ref[owner, q] = mixed[owner * depth : (owner + 1) * depth]


def mix(rp_coords, q_coords, modes, table, owners):
    e_local, r_local, both = table.shape
    width = both // 2
    block = 16
    out_shape = (owners, Q, width // owners, 2 * e_local)
    return pl.pallas_call(
        mix_kernel,
        grid=(e_local // block,),
        in_specs=[
            pl.BlockSpec(rp_coords.shape, lambda i: (0, 0)),
            pl.BlockSpec(q_coords.shape, lambda i: (0, 0)),
            pl.BlockSpec(modes.shape, lambda i: (0, 0, 0)),
            pl.BlockSpec((block, r_local, both), lambda i: (i, 0, 0)),
        ],
        out_specs=pl.BlockSpec(out_shape, lambda i: (0, 0, 0, 0)),
        out_shape=jax.ShapeDtypeStruct(out_shape, BF16),
        scratch_shapes=[
            pltpu.VMEM((Q, 2 * e_local, width), BF16),
            pltpu.VMEM((Q, width, width), BF16),
            pltpu.VMEM((2, Q * 2 * GROUP, GROUP * r_local), BF16),
        ],
        compiler_params=pltpu.CompilerParams(vmem_limit_bytes=50 << 20),
    )(rp_coords, q_coords, modes, table)


MESH = pl.DeviceIdType.MESH


def send(source, target, send_sem, recv_sem, device):
    return pltpu.make_async_remote_copy(
        src_ref=source, dst_ref=target, send_sem=send_sem, recv_sem=recv_sem,
        device_id=device, device_id_type=MESH,
    )


def bloch_kernel(
    partial_ref, near_ref, re_ref, k_ref, owner_ref, row_ref, out_ref,
    coupling_ref, all_ref, inbox, cosine, sine, summed, near, far,
    sum_send, sum_recv, far_send, far_recv, pair_send, pair_recv,
):
    shares = partial_ref.shape[0]
    devices, _, depth, twice = coupling_ref.shape
    half = devices // 2
    e_local = twice // 2
    k_local = k_ref.shape[1]
    pairs = NB * NB
    modes_local = depth // pairs
    chunks = Q * modes_local
    me, place = lax.axis_index("re"), lax.axis_index("rp")
    mate = me ^ 1

    barrier = pltpu.get_barrier_semaphore()
    peers = [(me, lax.rem(place + j, shares)) for j in range(1, shares)]
    peers += [(me ^ (2 * j), place) for j in range(1, half)] + [(mate, place)]
    for peer in peers:
        pl.semaphore_signal(barrier, inc=1, device_id=peer, device_id_type=MESH)
    pl.semaphore_wait(barrier, len(peers))

    def piece(c):
        q, v = divmod(c, modes_local)
        return q, pl.ds(v * pairs, pairs)

    sums = {}
    for c in range(chunks):
        at = piece(c)
        for j in range(1, shares):
            to = lax.rem(place + j, shares)
            copy = send(
                partial_ref.at[(to,) + at], inbox.at[(j - 1,) + at],
                sum_send.at[c, j - 1], sum_recv.at[c, j - 1], (me, to),
            )
            copy.start()
            sums[c, j] = copy

    spreads, waits, wholes = {}, {}, {}

    def spread(c, block, whole):
        wholes[c] = whole
        spreads[c] = []
        copy = send(block, whole(me), pair_send.at[c, 0], pair_recv.at[c, 0], (mate, place))
        for j in range(1, half):
            far_copy = send(
                block, whole(me), far_send.at[c, j], far_recv.at[c, j], (me ^ (2 * j), place)
            )
            far_copy.start()
            spreads[c].append(far_copy)
        copy.start()
        waits[c] = [copy]

    def forward(c):
        for j in range(1, half):
            spreads[c][j - 1].wait()
            block = wholes[c](me ^ (2 * j))
            copy = send(block, block, pair_send.at[c, j], pair_recv.at[c, j], (mate, place))
            copy.start()
            waits[c].append(copy)

    def collect(c):
        for copy in waits[c]:
            copy.wait()

    def add_up(c):
        at = piece(c)
        total = partial_ref[(place,) + at].astype(F32)
        for j in range(1, shares):
            sums[c, j].wait()
            total = total + inbox[(j - 1,) + at].astype(F32)
        coupling_ref[(me,) + at] = total.astype(BF16)
        whole = lambda d: coupling_ref.at[(d,) + at]
        spread(c, whole(me), whole)

    near[...] = near_ref[...].astype(F32).T
    all_ref[me] = near[...].astype(BF16)
    spread(chunks, all_ref.at[me], lambda d: all_ref.at[d])

    e_share = min(128, re_ref.shape[1])

    @pl.loop(0, re_ref.shape[1] // e_share)
    def _(d):
        start = pl.multiple_of(d * e_share, e_share)
        cos_k, sin_k = cycle(
            inner(narrow(re_ref[:, pl.ds(start, e_share)]), narrow(k_ref[...])) * (1.0 / GRID)
        )
        cosine[pl.ds(start, e_share), :] = cos_k
        sine[pl.ds(start, e_share), :] = sin_k

    def look_up(q):
        rows = lax.broadcasted_iota(jnp.int32, (k_local, k_local), 0)
        hot = (rows == row_ref[q : q + 1, :]).astype(F32).astype(BF16)
        owner = owner_ref[q : q + 1, :]
        far[q] = jnp.zeros(far.shape[1:], F32)

        @pl.loop(0, devices)
        def _(d):
            found = jnp.dot(all_ref[d], hot, preferred_element_type=F32)
            far[q] = jnp.where(owner == d, found, far[q])

    tile = min(256, k_local)
    lanes = 128

    def compute(c):
        q, v = divmod(c, modes_local)
        at = (q, pl.ds(v * pairs, pairs))
        left = jnp.concatenate(
            [
                jnp.concatenate(
                    [coupling_ref[(d,) + at][:, i * e_local : (i + 1) * e_local]
                     for d in range(devices)], axis=1,
                )
                for i in range(2)
            ],
            axis=0,
        )

        @pl.loop(0, k_local // tile)
        def _(j):
            cols = pl.ds(pl.multiple_of(j * tile, tile), tile)
            with_cos = jnp.dot(left, cosine[:, cols], preferred_element_type=F32)
            with_sin = jnp.dot(left, sine[:, cols], preferred_element_type=F32)
            summed[0, :, cols] = with_cos[:pairs] - with_sin[pairs:]
            summed[1, :, cols] = with_cos[pairs:] + with_sin[:pairs]

        @pl.loop(0, k_local // lanes)
        def _(i):
            cols = pl.ds(pl.multiple_of(i * lanes, lanes), lanes)

            def fill(ref, lead, row):
                return jnp.broadcast_to(ref[lead, pl.ds(row, 1), cols], (NB, lanes))

            right_real = [near[pl.ds(b * NB, NB), cols] for b in range(NB)]
            right_imag = [near[pl.ds(pairs + b * NB, NB), cols] for b in range(NB)]
            half_real, half_imag = [], []
            for a in range(NB):
                real = imag = None
                for b in range(NB):
                    c_real = fill(summed, 0, a * NB + b)
                    c_imag = fill(summed, 1, a * NB + b)
                    one = c_real * right_real[b] - c_imag * right_imag[b]
                    two = c_real * right_imag[b] + c_imag * right_real[b]
                    real = one if real is None else real + one
                    imag = two if imag is None else imag + two
                half_real.append(real)
                half_imag.append(imag)
            for m in range(0, NB, 2):
                reals, imags = [], []
                for n in (m, m + 1):
                    real = imag = None
                    for a in range(NB):
                        l_real = fill(far, q, a * NB + n)
                        l_imag = fill(far, q, pairs + a * NB + n)
                        one = l_real * half_real[a] + l_imag * half_imag[a]
                        two = l_real * half_imag[a] - l_imag * half_real[a]
                        real = one if real is None else real + one
                        imag = two if imag is None else imag + two
                    reals.append(real)
                    imags.append(imag)
                rows = pl.ds(m * NB, 2 * NB)
                out_ref[q, v, 0, rows, cols] = jnp.concatenate(reals, axis=0).astype(BF16)
                out_ref[q, v, 1, rows, cols] = jnp.concatenate(imags, axis=0).astype(BF16)

    lag = 3
    for t in range(chunks + lag):
        if t < chunks:
            add_up(t)
        if t == 0:
            forward(chunks)
        elif t <= chunks:
            forward(t - 1)
        if t == 1:
            collect(chunks)
        if 1 <= t <= Q:
            look_up(t - 1)
        if t >= lag:
            collect(t - lag)
            compute(t - lag)


def bloch(partial, near, re_rows, k_cols, owner, row, devices):
    shares, _, depth, twice = partial.shape
    e_all = re_rows.shape[1]
    k_local = k_cols.shape[1]
    pairs = NB * NB
    modes_local = depth // pairs
    chunks = Q * modes_local
    half = devices // 2
    return pl.pallas_call(
        bloch_kernel,
        in_specs=[pl.BlockSpec(memory_space=pltpu.VMEM)] * 6,
        out_specs=pl.BlockSpec(memory_space=pltpu.VMEM),
        out_shape=jax.ShapeDtypeStruct((Q, modes_local, 2, pairs, k_local), BF16),
        scratch_shapes=[
            pltpu.VMEM((devices, Q, depth, twice), BF16),
            pltpu.VMEM((devices, 2 * pairs, k_local), BF16),
            pltpu.VMEM((shares - 1, Q, depth, twice), BF16),
            pltpu.VMEM((e_all, k_local), BF16),
            pltpu.VMEM((e_all, k_local), BF16),
            pltpu.VMEM((2, pairs, k_local), F32),
            pltpu.VMEM((2 * pairs, k_local), F32),
            pltpu.VMEM((Q, 2 * pairs, k_local), F32),
            pltpu.SemaphoreType.DMA((chunks, shares - 1)),
            pltpu.SemaphoreType.DMA((chunks, shares - 1)),
            pltpu.SemaphoreType.DMA((chunks + 1, half)),
            pltpu.SemaphoreType.DMA((chunks + 1, half)),
            pltpu.SemaphoreType.DMA((chunks + 1, half)),
            pltpu.SemaphoreType.DMA((chunks + 1, half)),
        ],
        compiler_params=pltpu.CompilerParams(
            collective_id=0, has_side_effects=True, vmem_limit_bytes=40 << 20
        ),
    )(partial, near, re_rows, k_cols, owner, row)


def local(
    wannier_table,
    mode_matrix,
    re_coords,
    rp_coords,
    q_coords,
    k_coords,
    rotations,
    kq_owner,
    kq_row,
):
    k_local = k_coords.shape[1]
    devices, shares = lax.axis_size("re"), lax.axis_size("rp")
    partial = mix(rp_coords, q_coords, mode_matrix, wannier_table, shares)
    owner = kq_owner.reshape(Q, k_local)
    return bloch(partial, rotations, re_coords, k_coords, owner, kq_row, devices)


def solution(mesh):
    in_specs = (
        P("re", "rp", None),
        P(),
        P(),
        P(None, "rp"),
        P(),
        P(None, "re"),
        P("re", None),
        P(None, "re", None),
        P(None, "re"),
    )
    out_specs = P(None, "rp", None, None, "re")
    return jax.shard_map(local, mesh=mesh, in_specs=in_specs, out_specs=out_specs, check_vma=False)
```
